32 devices in a mesh: parts: 16 (over z, y, core), mp: 2 (over x).
Axes of the slice: x: 2, y: 2, z: 4, core: 2. Of those that a mesh axis runs over, the one named last changes fastest.
Arguments:
- feats: bfloat16 [2048, 1024], P('parts', 'mp'), may hold values from -6 to 6
- adj_local: bfloat16 [2048, 128], P('parts'), may hold values from -0.5 to 0.5
- adj_halo: bfloat16 [2048, 128], P('parts'), may hold values from -0.5 to 0.5
- w_graph: bfloat16 [1024, 1024], P(None, 'mp'), may hold values from -0.1875 to 0.1875
- w_query: bfloat16 [1024, 1024], P(None, 'mp'), may hold values from -0.1875 to 0.1875
- w_key: bfloat16 [1024, 1024], P(None, 'mp'), may hold values from -0.1875 to 0.1875
- w_value: bfloat16 [1024, 1024], P(None, 'mp'), may hold values from -0.1875 to 0.1875
- send_rows: int32 [16, 16, 8], P('parts'), may hold values from 0 to 127
- send_count: int32 [16, 16], P('parts'), may hold values from 0 to 8
- live: int32 [16], P('parts'), may hold values from 64 to 128
Outputs:
- attended: float32 [2048, 1024], P('parts', 'mp')
- key_summary: float32 [1024, 1024], P('mp')
The draws below stay inside these ranges and needn't reach their ends.
All inputs are finite; a program needn't handle non-finite values.
Results may differ from the reference program's by a relative error of at most 0.0029.
The reference program's roundings to bfloat16 on the way count: a program that leaves them out, or rounds other values in their place, can miss the bound.
Values may be sent and summed in bfloat16 or wider, within the bound.
A program may use at most 64 MiB of HBM per device.

```python
import math
import jax
import jax.numpy as jnp
from jax import lax

D = 1024
ROWS = 128
BLK = 8
NODES = 2048
SLOTS = 128
N_PARTS = 16


def set_ends(drawn, key, smallest, high):
    index_at = [jax.random.randint(jax.random.fold_in(key, axis), (), 0, length) for axis, length in enumerate(drawn.shape)]
    main_axis = drawn.shape.index(max(drawn.shape))
    neighbour = index_at[:main_axis] + [(index_at[main_axis] + 1) % drawn.shape[main_axis]] + index_at[main_axis + 1:]
    return drawn.at[tuple(index_at)].set(smallest).at[tuple(neighbour)].set(high)


def levels(rng, dims, split, low, high):
    gain = 1.0
    for dim, blocks in split:
        draws = jax.random.uniform(jax.random.fold_in(jax.random.fold_in(rng, 6), dim), (blocks,), jnp.float32, low / len(split), high / len(split))
        gain = gain * jnp.repeat(jnp.exp(draws), dims[dim] // blocks).reshape((-1,) + (1,) * (len(dims) - 1 - dim))
    return gain


def normal_values(key, shape, deviation, bound, cuts=(), held_as=jnp.bfloat16):
    entries = deviation * jax.random.normal(key, shape, jnp.float32)
    if cuts:
        entries = entries * levels(key, shape, cuts, -0.22, 0.18)
    return jnp.clip(entries, -bound, bound).astype(held_as)


def setup_inputs(seed: int = 0) -> dict:
    splits = jax.random.split(jax.random.key(seed), 11)
    return {
        "feats": normal_values(splits[0], (NODES, D), 1.0, 6.0, ((0, 16), (1, 2))),
        "adj_local": normal_values(splits[1], (NODES, ROWS), ROWS ** -0.5, 0.5, ((0, 16),)),
        "adj_halo": normal_values(splits[2], (NODES, SLOTS), SLOTS ** -0.5, 0.5, ((0, 16),)),
        "w_graph": normal_values(splits[3], (D, D), D ** -0.5, 0.1875, ((1, 2),)),
        "w_query": normal_values(splits[4], (D, D), D ** -0.5, 0.1875, ((1, 2),)),
        "w_key": normal_values(splits[5], (D, D), D ** -0.5, 0.1875, ((1, 2),)),
        "w_value": normal_values(splits[6], (D, D), D ** -0.5, 0.1875, ((1, 2),)),
        "send_rows": set_ends(jax.random.randint(splits[7], (N_PARTS, N_PARTS, BLK), 0, ROWS), jax.random.fold_in(splits[7], 1), 0, ROWS - 1).astype(jnp.int32),
        "send_count": set_ends(jax.random.randint(splits[8], (N_PARTS, N_PARTS), 0, BLK + 1), jax.random.fold_in(splits[8], 1), 0, BLK).astype(jnp.int32),
        "live": set_ends(jax.random.randint(splits[9], (N_PARTS,), ROWS // 2, ROWS + 1), jax.random.fold_in(splits[9], 1), ROWS // 2, ROWS).astype(jnp.int32),
    }


def reference(feats, adj_local, adj_halo, w_graph, w_query, w_key, w_value, send_rows, send_count, live):
    width_all = feats.shape[1]
    feat_blocks = feats.reshape(N_PARTS, ROWS, width_all)
    local_tiles = adj_local.reshape(N_PARTS, ROWS, ROWS)
    halo_tiles = adj_halo.reshape(N_PARTS, ROWS, SLOTS)
    slot_ids = jnp.arange(BLK, dtype=jnp.int32)
    part_ids = jnp.arange(N_PARTS, dtype=jnp.int32)

    def one_part(part_index):
        own_rows = feat_blocks[part_index]
        source_rows = send_rows[:, part_index, :]
        counts = send_count[:, part_index]
        picked = feat_blocks[part_ids[:, None], source_rows]
        picked = jnp.where((slot_ids[None, :] < counts[:, None])[:, :, None], picked, jnp.zeros((), jnp.bfloat16))
        summed = jnp.dot(local_tiles[part_index], own_rows, preferred_element_type=jnp.float32)
        summed = summed + jnp.dot(halo_tiles[part_index], picked.reshape(SLOTS, width_all), preferred_element_type=jnp.float32)
        return summed.astype(jnp.bfloat16)
    convolved = lax.map(one_part, part_ids).reshape(NODES, width_all)
    hidden = jax.nn.gelu(jnp.dot(convolved, w_graph, preferred_element_type=jnp.float32), approximate=False).astype(jnp.bfloat16)
    live_mask = (jnp.arange(ROWS, dtype=jnp.int32)[None, :] < live[:, None]).reshape(NODES, 1)
    queries = jnp.dot(hidden, w_query, preferred_element_type=jnp.float32)
    keys_raw = jnp.dot(hidden, w_key, preferred_element_type=jnp.float32)
    query_feat = jnp.where(live_mask, jax.nn.elu(queries) + 1.0, 0.0).astype(jnp.bfloat16)
    key_feat = jnp.where(live_mask, jax.nn.elu(keys_raw) + 1.0, 0.0).astype(jnp.bfloat16)
    values = jnp.dot(hidden, w_value, preferred_element_type=jnp.float32).astype(jnp.bfloat16)
    query_wide = query_feat.astype(jnp.float32)
    key_wide = key_feat.astype(jnp.float32)
    query_sq = jnp.sum(query_wide * query_wide)
    key_sq = jnp.sum(key_wide * key_wide)
    key_values = lax.dot_general(key_feat, values, (((0,), (0,)), ((), ())), preferred_element_type=jnp.float32)
    key_total = lax.optimization_barrier(jnp.sum(key_wide, axis=0))
    key_summary = key_values / math.sqrt(NODES)
    key_values_b = key_values.astype(jnp.bfloat16)
    numerator = jnp.dot(query_feat, key_values_b, preferred_element_type=jnp.float32)
    denominator = jnp.dot(query_wide, key_total, precision=lax.Precision.HIGHEST)
    inverse = lax.rsqrt(query_sq) * lax.rsqrt(key_sq)
    result = (values.astype(jnp.float32) + numerator * inverse) / (1.0 + denominator * inverse)[:, None]
    return (jnp.where(live_mask, result, 0.0), key_summary)
```

```python
import functools
import math

import jax
import jax.numpy as jnp
from jax import lax
from jax.experimental import pallas as pl
from jax.experimental.pallas import tpu as pltpu
from jax.sharding import PartitionSpec as P

MESH = pl.DeviceIdType.MESH
F32 = jnp.float32
BF16 = jnp.bfloat16


def plain(
    feats, adj_local, adj_halo, w_graph, w_query, w_key, w_value, send_rows, send_count, live
):
    row_count, col_count = feats.shape
    slot_count = send_rows.shape[2]
    picked = feats[send_rows[0]]
    slot_live = jnp.arange(slot_count, dtype=jnp.int32)[None, :] < send_count[0][:, None]
    outgoing = jnp.where(slot_live[:, :, None], picked, jnp.zeros((), jnp.bfloat16))
    incoming = lax.all_to_all(outgoing, "parts", split_axis=0, concat_axis=0, tiled=True)
    halo_rows = incoming.reshape(-1, col_count)
    summed = jnp.dot(adj_local, feats, preferred_element_type=jnp.float32)
    summed = summed + jnp.dot(adj_halo, halo_rows, preferred_element_type=jnp.float32)
    convolved = summed.astype(jnp.bfloat16)
    out_cols = w_graph.shape[1]
    empty = jnp.zeros((row_count, out_cols), jnp.float32)
    weight_rows = w_graph
    projected = jnp.dot(
        lax.all_gather(convolved, "mp", axis=1, tiled=True),
        weight_rows,
        preferred_element_type=jnp.float32,
    )
    hidden = jax.nn.gelu(projected, approximate=False).astype(jnp.bfloat16)
    totals = (empty, empty, empty)
    portion = lax.all_gather(hidden, "mp", axis=1, tiled=True)
    outputs = []
    for running, weight in zip(totals, (w_query, w_key, w_value)):
        weight_rows = weight
        outputs.append(jnp.dot(portion, weight_rows, preferred_element_type=jnp.float32))
    queries, keys_raw, values_wide = tuple(outputs)
    live_mask = jnp.arange(row_count, dtype=jnp.int32)[:, None] < live[0]
    query_feat = jnp.where(live_mask, jax.nn.elu(queries) + 1.0, 0.0).astype(jnp.bfloat16)
    key_feat = jnp.where(live_mask, jax.nn.elu(keys_raw) + 1.0, 0.0).astype(jnp.bfloat16)
    values = values_wide.astype(jnp.bfloat16)
    key_values = lax.dot_general(
        key_feat,
        lax.all_gather(values, "mp", axis=1, tiled=True),
        (((0,), (0,)), ((), ())),
        preferred_element_type=jnp.float32,
    )
    query_wide = query_feat.astype(jnp.float32)
    key_wide = key_feat.astype(jnp.float32)
    key_total = jnp.sum(key_wide, axis=0)
    sq_pair = jnp.stack([jnp.sum(query_wide * query_wide), jnp.sum(key_wide * key_wide)])
    key_values, key_total, sq_pair = lax.psum((key_values, key_total, sq_pair), "parts")
    key_summary = key_values / math.sqrt(lax.axis_size("parts") * row_count)
    numer_part = jnp.dot(
        query_feat, key_values.astype(jnp.bfloat16), preferred_element_type=jnp.float32
    )
    denom_part = jnp.dot(query_wide, key_total, precision=lax.Precision.HIGHEST)
    numerator = lax.psum_scatter(
        numer_part.astype(jnp.bfloat16), "mp", scatter_dimension=1, tiled=True
    ).astype(jnp.float32)
    denominator, sq_pair = lax.psum((denom_part, sq_pair), "mp")
    inverse = lax.rsqrt(sq_pair[0]) * lax.rsqrt(sq_pair[1])
    result = (values.astype(jnp.float32) + numerator * inverse) / (1.0 + denominator * inverse)[
        :, None
    ]
    return (jnp.where(live_mask, result, 0.0), key_summary)


def dot(a, b):
    return jnp.dot(a, b, preferred_element_type=F32)


def kernel(
    n,
    chunks,
    feats_in,
    adj_local_in,
    adj_halo_in,
    send_rows_in,
    send_count_in,
    live,
    wg,
    wq,
    wk,
    wv,
    out,
    kv_out,
    feats,
    adj_local,
    adj_halo,
    send_rows,
    send_count,
    wbuf,
    outgoing,
    incoming,
    conv,
    hid,
    val,
    query,
    keyb,
    keyx,
    queryb,
    queryx,
    tbuf,
    ysend,
    yrecv,
    acc,
    zsend,
    zrecv,
    kvl,
    kvs,
    kvx,
    kvxs,
    nsend,
    nrecv,
    stat,
    den,
    isem,
    wsem,
    osem,
    feat_sem,
    halo_s,
    halo_r,
    fwd_s,
    fwd_r,
    hid_sem,
    key_s,
    key_r,
    query_s,
    query_r,
    val_sem,
    num_s,
    num_r,
    y_s,
    y_r,
    z_s,
    z_r,
    g_s,
    g_r,
    gy_s,
    gy_r,
    gx_s,
    gx_r,
    gc_s,
    gc_r,
    gd_s,
    gd_r,
    st_s,
    st_r,
    den_sem,
):
    p = lax.axis_index("parts")
    m = lax.axis_index("mp")
    c, y, z = p % 2, (p // 2) % 2, p // 4
    other = 1 - m
    sibling = p + 1 - 2 * c
    y_peer = p + 2 - 4 * y
    rows, cols = feats.shape[1:]
    slots = outgoing.shape[1]
    total = n * slots
    half, piece = cols // 2, zrecv.shape[2]
    width = zrecv.shape[3]
    groups = cols // width

    z_near = z + 1 - 2 * (z % 2)
    z_far = lax.rem(z + 2, 4)
    z_mirror = 3 - z
    edge = jnp.logical_or(z == 0, z == 3)
    inner = jnp.logical_not(edge)

    def spot_of(yy, zz):
        return pl.ds(pl.multiple_of((yy * 4 + zz) * piece, piece), piece)

    def make(src, dst, s_sem, r_sem, device):
        return pltpu.make_async_remote_copy(
            src_ref=src,
            dst_ref=dst,
            send_sem=s_sem,
            recv_sem=r_sem,
            device_id=device,
            device_id_type=MESH,
        )

    def send(src, dst, s_sem, r_sem, device):
        copy = make(src, dst, s_sem, r_sem, device)
        copy.start()
        return copy

    def wait_for(like, sem):
        pltpu.make_async_copy(like, like, sem).wait()

    inputs = []
    for i, (source, place) in enumerate(
        (
            (send_rows_in, send_rows),
            (send_count_in, send_count),
            (feats_in, feats.at[m]),
            (adj_local_in, adj_local),
            (adj_halo_in, adj_halo),
        )
    ):
        load = pltpu.make_async_copy(source, place, isem.at[i])
        load.start()
        inputs.append(load)
    loads = []
    for i, w in enumerate((wg, wk, wv, wq)):
        load = pltpu.make_async_copy(w, wbuf.at[i], wsem.at[i])
        load.start()
        loads.append(load)

    barrier = pltpu.get_barrier_semaphore()
    for d in range(1, n):
        pl.semaphore_signal(
            barrier, inc=1, device_id={"parts": lax.rem(p + d, n)}, device_id_type=MESH
        )
    for to in (p, sibling, y_peer):
        pl.semaphore_signal(
            barrier, inc=1, device_id={"parts": to, "mp": other}, device_id_type=MESH
        )

    for load in inputs:
        load.wait()

    owner = lax.broadcasted_iota(jnp.int32, (total, n), 0) // slots
    is_owner = owner == lax.broadcasted_iota(jnp.int32, (total, n), 1)
    spot = lax.broadcasted_iota(jnp.int32, (total, slots), 0) % slots
    is_spot = spot == lax.broadcasted_iota(jnp.int32, (total, slots), 1)
    spread = lax.dot_general(
        is_owner.astype(F32),
        send_rows[...].astype(F32),
        (((1,), (1,)), ((), ())),
        precision=lax.Precision.HIGHEST,
        preferred_element_type=F32,
    )
    index = jnp.sum(jnp.where(is_spot, spread, 0.0), axis=1, keepdims=True)
    count = jnp.sum(
        jnp.where(is_owner, send_count[...].astype(F32), 0.0), axis=1, keepdims=True
    )
    slot_id = jnp.sum(
        jnp.where(is_spot, lax.broadcasted_iota(jnp.int32, (total, slots), 1), 0).astype(F32),
        axis=1,
        keepdims=True,
    )
    index = jnp.where(slot_id < count, index, -1.0)
    node = lax.broadcasted_iota(jnp.int32, (total, rows), 1).astype(F32)
    pick = jnp.where(index == node, 1.0, 0.0).astype(BF16)
    outgoing[...] = dot(pick, feats[m]).reshape(n, slots, cols).astype(BF16)

    def partner(k):
        kz, ky, kc = k // 4, (k // 2) % 2, k % 2
        zz = (z, z_near, z_far, z_mirror)[kz]
        yy = 1 - y if ky else y
        cc = 1 - c if kc else c
        return zz * 4 + yy * 2 + cc

    pl.semaphore_wait(barrier, n + 2)
    for k in (*range(12, n), *range(8, 12), *range(4, 8), *range(1, 4)):
        to = partner(k)
        send(outgoing.at[to], incoming.at[m, p], halo_s, halo_r.at[k // 4], {"parts": to})
    swap_feats = send(feats.at[m], feats.at[m], feat_sem.at[0], feat_sem.at[1], {"mp": other})
    send(outgoing.at[p], incoming.at[m, p], fwd_s, fwd_r, {"mp": other})
    incoming[m, p] = outgoing[p]
    local_mine = dot(adj_local[...], feats[m])
    for kz in range(4):
        members = range(max(1, 4 * kz), 4 * kz + 4)
        wait_for(outgoing.at[pl.ds(0, len(members))], halo_r.at[kz])
        for k in members:
            block = incoming.at[m, partner(k)]
            send(block, block, fwd_s, fwd_r, {"mp": other})

    def convolve(side, local_sum):
        arrived = incoming[side].astype(F32).reshape(total, cols).astype(BF16)
        conv[side] = (local_sum + dot(adj_halo[...], arrived)).astype(BF16)

    mine = pl.ds(pl.multiple_of(m * cols, cols), cols)
    theirs = pl.ds(pl.multiple_of(other * cols, cols), cols)
    convolve(m, local_mine)
    loads[0].wait()
    projected = dot(conv[m], wbuf[0, mine, :])
    swap_feats.wait_recv()
    local_theirs = dot(adj_local[...], feats[other])
    wait_for(outgoing, fwd_r)
    convolve(other, local_theirs)
    projected = projected + dot(conv[other], wbuf[0, theirs, :])
    hid[m] = (0.5 * projected * (1.0 + lax.erf(projected * math.sqrt(0.5)))).astype(BF16)
    swap = send(hid.at[m], hid.at[m], hid_sem.at[0], hid_sem.at[1], {"mp": other})
    for load in loads[1:]:
        load.wait()
    own = hid[m]
    raw_k = dot(own, wbuf[1, mine, :])
    raw_v = dot(own, wbuf[2, mine, :])
    raw_q = dot(own, wbuf[3, mine, :])
    live_mask = lax.broadcasted_iota(jnp.int32, (rows, 1), 0) < live[0]

    def feature(x):
        x = jnp.where(x > 0.0, x + 1.0, jnp.exp(jnp.minimum(x, 0.0)))
        return jnp.where(live_mask, x, 0.0).astype(BF16)

    def spread_blocks(blocks, place, s_sems, r_sems):
        away = blocks.at[1 - c]
        return [
            send(blocks.at[c], place.at[1, c], s_sems.at[0], r_sems.at[0], {"mp": other}),
            send(
                away,
                place.at[1, c],
                s_sems.at[1],
                r_sems.at[1],
                {"parts": sibling, "mp": other},
            ),
            send(away, place.at[0, c], s_sems.at[2], r_sems.at[2], {"parts": sibling}),
        ]

    swap.wait_recv()
    rest = hid[other]
    key_feat = feature(raw_k + dot(rest, wbuf[1, theirs, :]))
    key_wide = key_feat.astype(F32)
    key_t = key_wide.T.astype(BF16)
    for b in range(2):
        keyb[b] = key_t[b * half : (b + 1) * half]
    keys = spread_blocks(keyb, keyx, key_s, key_r)
    val[c] = (raw_v + dot(rest, wbuf[2, theirs, :])).astype(BF16)
    values = send(val.at[c], val.at[c], val_sem.at[0], val_sem.at[1], {"parts": sibling})
    query_feat = feature(raw_q + dot(rest, wbuf[3, theirs, :]))
    query[...] = query_feat
    for b in range(2):
        queryb[b] = query_feat[:, b * half : (b + 1) * half]
    query_wide = query_feat.astype(F32)
    lane = lax.broadcasted_iota(jnp.int32, (1, 128), 1)
    query_sq = jnp.sum(jnp.sum(query_wide * query_wide, axis=0, keepdims=True), axis=1, keepdims=True)
    key_sq = jnp.sum(jnp.sum(key_wide * key_wide, axis=0, keepdims=True), axis=1, keepdims=True)
    stat[0, :, :cols] = jnp.sum(key_wide, axis=0, keepdims=True)
    stat[0, :, cols:] = jnp.where(lane == 0, query_sq, jnp.where(lane == 1, key_sq, 0.0))
    for k in range(1, n):
        send(stat.at[0], stat.at[k], st_s, st_r, {"parts": partner(k)})
    queries = spread_blocks(queryb, queryx, query_s, query_r)

    y_copies, numer = {}, {}

    def product(i):
        a, g = chunks[i]
        columns = pl.ds(g * width, width)
        if a == 0:
            first, second = keyb[c], keyx[0, 1 - c]
        else:
            first, second = keyx[1, c], keyx[1, 1 - c]
        whole = dot(first, val[c, :, columns]) + dot(second, val[1 - c, :, columns])
        tbuf[i] = whole.reshape(2, 4 * piece, width)
        ysend[i] = tbuf[i, 1 - y].astype(BF16)
        y_copies[i] = send(ysend.at[i], yrecv.at[i], y_s, y_r.at[i], {"parts": y_peer})

    def on_z(zz):
        return {"parts": zz * 4 + p % 4}

    z_copies, g_copies = {}, {}

    def z_send(i):
        y_copies[i].wait_recv()
        acc[i] = (tbuf[i, y] + yrecv[i].astype(F32)).reshape(4, piece, width)
        zsend[i] = acc[i].astype(BF16)
        near, mirror, far = range(3)
        z_copies[i] = [
            send(
                zsend.at[i, z_near],
                zrecv.at[i, near],
                z_s,
                z_r.at[i, 0],
                on_z(z_near),
            ),
            make(
                zsend.at[i, z_mirror],
                zrecv.at[i, mirror],
                z_s,
                z_r.at[i, 0],
                on_z(z_mirror),
            ),
        ]
        z_copies[i].append(
            send(
                zsend.at[i, z_far],
                zrecv.at[i, far],
                z_s,
                z_r.at[i, 1],
                on_z(jnp.where(edge, z_near, z_far)),
            )
        )

        @pl.when(edge)
        def _():
            z_copies[i][1].start()

    def z_combine(i):
        @pl.when(inner)
        def _():
            z_copies[i][2].wait_recv()
            zsend[i, z_mirror] = (acc[i, z_mirror] + zrecv[i, 2].astype(F32)).astype(BF16)
            z_copies[i][1].start()

    def pass_on(i, zz):
        place = kvl.at[i, spot_of(y, zz)]
        send(place, place, gy_s, gy_r.at[i], {"parts": y_peer})
        if chunks[i][0] == 1:
            g = chunks[i][1]
            target = kvx.at[g, spot_of(y, zz)]
            send(place, target, gx_s, gx_r.at[g], {"mp": other})
            send(place, target, gx_s, gx_r.at[g], {"parts": y_peer, "mp": other})

    def z_final(i):
        @pl.when(edge)
        def _():
            z_copies[i][2].wait_recv()

        wait_for(zrecv.at[i, pl.ds(0, 2)], z_r.at[i, 0])
        final = acc[i, z] + zrecv[i, 0].astype(F32) + zrecv[i, 1].astype(F32)
        final = final + jnp.where(edge, zrecv[i, 2].astype(F32), 0.0)
        place = kvl.at[i, spot_of(y, z)]
        place[...] = final.astype(BF16)
        g_copies[i] = [
            send(place, place, g_s, g_r.at[i, 0], on_z(z_near)),
            send(place, place, g_s, g_r.at[i, 1], on_z(z_mirror)),
            make(place, place, g_s, g_r.at[i, 2], on_z(z_far)),
        ]

        @pl.when(edge)
        def _():
            g_copies[i][2].start()

        pass_on(i, z)

    def z_gather_first(i):
        @pl.when(inner)
        def _():
            g_copies[i][1].wait_recv()
            place = kvl.at[i, spot_of(y, z_mirror)]
            send(place, place, g_s, g_r.at[i, 2], on_z(z_near))
            pass_on(i, z_mirror)

        g_copies[i][0].wait_recv()
        pass_on(i, z_near)

    def z_gather_last(i):
        @pl.when(edge)
        def _():
            g_copies[i][1].wait_recv()
            pass_on(i, z_mirror)

        g_copies[i][2].wait_recv()
        pass_on(i, z_far)

    num_copies = {}

    def store(place, core, side, g):
        target = kv_out.at[
            pl.ds(pl.multiple_of(core * half, half), half),
            pl.ds(pl.multiple_of(side * cols + g * width, width), width),
        ]
        pltpu.make_async_copy(place, target, osem).start()

    def y_gather(i):
        a, g = chunks[i]
        wait_for(yrecv.at[i], gy_r.at[i])
        if a == 0:
            send(
                kvl.at[i], kvs.at[g], gc_s, gc_r, {"parts": sibling}
            )
        block = kvl[i]
        if a == 0:
            numer[g] = [dot(queryb[c], block), dot(queryx[0, 1 - c], block)]
        else:
            nsend[g] = numer[g][1] + dot(queryx[1, 1 - c], block)
            num_copies[g] = send(
                nsend.at[g], nrecv.at[g], num_s, num_r.at[g], {"parts": sibling}
            )
            numer[g] = numer[g][0] + dot(queryx[1, c], block)

    def denominators():
        wait_for(stat.at[pl.ds(1, n - 1)], st_r)
        sums = stat[0]
        for k in range(1, n):
            sums = sums + stat[k]
        den[m, :rows, :] = jnp.broadcast_to(
            jnp.sum(query[...].astype(F32) * sums[:, :cols], axis=1, keepdims=True),
            (rows, 128),
        )
        den[m, rows:, :] = jnp.broadcast_to(sums[:, cols:], (8, 128))
        return send(den.at[m], den.at[m], den_sem.at[0], den_sem.at[1], {"mp": other})

    keys[2].wait_recv()
    values.wait_recv()
    early = [i for i, (a, _) in enumerate(chunks) if a == 0]
    for i in early:
        product(i)
    for copy in keys[:2]:
        copy.wait_recv()
    for i in range(len(chunks)):
        if i not in early:
            product(i)

    plan = []
    for i in range(len(chunks)):
        t = 3.0 + 1.3 * i + (0.4 if chunks[i][0] else 0.0)
        plan += [
            (t, z_send, i),
            (t + 2.1, z_combine, i),
            (t + 4.3, z_final, i),
            (t + 8.5, z_gather_first, i),
            (t + 11.0, z_gather_last, i),
            (t + 13.0, y_gather, i),
        ]
    queried = False
    for t, step, i in sorted(plan, key=lambda entry: entry[0]):
        if step is y_gather and not queried:
            queried = True
            den_swap = denominators()
            for copy in queries:
                copy.wait_recv()
        step(i)

    den_swap.wait_recv()
    square = den[0, rows : rows + 1, :] + den[1, rows : rows + 1, :]
    query_sq = jnp.sum(jnp.where(lane == 0, square, 0.0), axis=1, keepdims=True)
    key_sq = jnp.sum(jnp.where(lane == 1, square, 0.0), axis=1, keepdims=True)
    inverse = lax.rsqrt(query_sq) * lax.rsqrt(key_sq)
    denominator = den[0, :rows, 0:1] + den[1, :rows, 0:1]
    scale = 1.0 + denominator * inverse

    for i in early:
        store(kvl.at[i], c, m, chunks[i][1])
    wait_for(kvs, gc_r)
    for g in range(groups):
        store(kvs.at[g], 1 - c, m, g)
    for g in range(groups):
        columns = pl.ds(g * width, width)
        num_copies[g].wait_recv()
        result = (val[c, :, columns].astype(F32) + (numer[g] + nrecv[g]) * inverse) / scale
        out[:, columns] = jnp.where(live_mask, result, 0.0)
    last = []
    for g in range(groups):
        wait_for(kvx.at[g], gx_r.at[g])
        last.append(
            send(kvx.at[g], kvxs.at[g], gd_s, gd_r.at[g], {"parts": sibling})
        )
        store(kvx.at[g], c, other, g)
    for g in range(groups):
        last[g].wait_recv()
        store(kvxs.at[g], 1 - c, other, g)

    wait_for(outgoing.at[pl.ds(0, n - 1)], halo_s)
    wait_for(outgoing, fwd_s)
    wait_for(stat.at[pl.ds(1, n - 1)], st_s)
    wait_for(ysend, y_s)
    wait_for(zrecv, z_s)
    wait_for(zrecv, g_s)
    wait_for(yrecv, gy_s)
    wait_for(kvx, gx_s)
    wait_for(kvs, gc_s)
    wait_for(kvx, gd_s)
    wait_for(nsend, num_s)
    for copy in (swap_feats, swap, *keys, values, *queries, den_swap):
        copy.wait_send()
    wait_for(kv_out, osem)


def fused(
    feats, adj_local, adj_halo, w_graph, w_query, w_key, w_value, send_rows, send_count, live
):
    n = lax.axis_size("parts")
    rows, cols = feats.shape
    slots = send_rows.shape[2]
    depth = w_graph.shape[0]
    half, piece = cols // 2, cols // 16
    groups = 2
    width = cols // groups
    chunks = tuple((a, g) for a in range(2) for g in range(groups))
    count = len(chunks)
    vmem = pl.BlockSpec(memory_space=pltpu.VMEM)
    hbm = pl.BlockSpec(memory_space=pltpu.HBM)
    dma = pltpu.SemaphoreType.DMA
    place = functools.partial(pltpu.with_memory_space_constraint, memory_space=pltpu.HBM)
    gathered = (half, width)
    out, kv = pl.pallas_call(
        functools.partial(kernel, n, chunks),
        out_shape=(
            jax.ShapeDtypeStruct((rows, cols), F32),
            jax.ShapeDtypeStruct((cols, depth), BF16),
        ),
        in_specs=[hbm] * 5 + [pl.BlockSpec(memory_space=pltpu.SMEM)] + [hbm] * 4,
        out_specs=(vmem, pl.BlockSpec(memory_space=pl.ANY)),
        scratch_shapes=[
            pltpu.VMEM((2, rows, cols), BF16),
            pltpu.VMEM(adj_local.shape, BF16),
            pltpu.VMEM(adj_halo.shape, BF16),
            pltpu.VMEM((slots, n), jnp.int32),
            pltpu.VMEM((1, n), jnp.int32),
            pltpu.VMEM((4, depth, cols), BF16),
            pltpu.VMEM((n, slots, cols), BF16),
            pltpu.VMEM((2, n, slots, cols), BF16),
            pltpu.VMEM((2, rows, cols), BF16),
            pltpu.VMEM((2, rows, cols), BF16),
            pltpu.VMEM((2, rows, cols), BF16),
            pltpu.VMEM((rows, cols), BF16),
            pltpu.VMEM((2, half, rows), BF16),
            pltpu.VMEM((2, 2, half, rows), BF16),
            pltpu.VMEM((2, rows, half), BF16),
            pltpu.VMEM((2, 2, rows, half), BF16),
            pltpu.VMEM((count, 2, 4 * piece, width), F32),
            pltpu.VMEM((count, 4 * piece, width), BF16),
            pltpu.VMEM((count, 4 * piece, width), BF16),
            pltpu.VMEM((count, 4, piece, width), F32),
            pltpu.VMEM((count, 4, piece, width), BF16),
            pltpu.VMEM((count, 3, piece, width), BF16),
            pltpu.VMEM((count, *gathered), BF16),
            pltpu.VMEM((groups, *gathered), BF16),
            pltpu.VMEM((groups, *gathered), BF16),
            pltpu.VMEM((groups, *gathered), BF16),
            pltpu.VMEM((groups, rows, width), F32),
            pltpu.VMEM((groups, rows, width), F32),
            pltpu.VMEM((n, 1, cols + 128), F32),
            pltpu.VMEM((2, rows + 8, 128), F32),
            dma((5,)),
            dma((4,)),
            dma,
            dma((2,)),
            dma,
            dma((4,)),
            dma,
            dma,
            dma((2,)),
            dma((3,)),
            dma((3,)),
            dma((3,)),
            dma((3,)),
            dma((2,)),
            dma,
            dma((groups,)),
            dma,
            dma((count,)),
            dma,
            dma((count, 2)),
            dma,
            dma((count, 3)),
            dma,
            dma((count,)),
            dma,
            dma((groups,)),
            dma,
            dma,
            dma,
            dma((groups,)),
            dma,
            dma,
            dma((2,)),
        ],
        compiler_params=pltpu.CompilerParams(
            collective_id=0, has_side_effects=True, vmem_limit_bytes=24 * 1024 * 1024
        ),
    )(
        *(place(a) for a in (feats, adj_local, adj_halo, send_rows[0].T, send_count)),
        live,
        *(place(w) for w in (w_graph, w_query, w_key, w_value)),
    )
    return out, kv.astype(F32) / math.sqrt(n * rows)


def local(*args):
    n = lax.axis_size("parts")
    rows, cols = args[0].shape
    slots = args[7].shape[2]
    fits = (
        lax.axis_size("mp") == 2
        and n == 16
        and cols % 256 == 0
        and rows % 128 == 0
        and (n * slots) % 16 == 0
        and slots % 8 == 0
    )
    return fused(*args) if fits else plain(*args)


def solution(mesh):
    return jax.shard_map(
        local,
        mesh=mesh,
        in_specs=(
            P("parts", "mp"),
            P("parts", None),
            P("parts", None),
            P(None, "mp"),
            P(None, "mp"),
            P(None, "mp"),
            P(None, "mp"),
            P("parts", None, None),
            P("parts", None),
            P("parts"),
        ),
        out_specs=(P("parts", "mp"), P("mp", None)),
        check_vma=False,
    )
```

```python
import functools
import math

import jax
import jax.numpy as jnp
from jax import lax
from jax.experimental import pallas as pl
from jax.experimental.pallas import tpu as pltpu
from jax.sharding import PartitionSpec as P

MESH = pl.DeviceIdType.MESH
F32 = jnp.float32
BF16 = jnp.bfloat16


def plain(
    feats, adj_local, adj_halo, w_graph, w_query, w_key, w_value, send_rows, send_count, live
):
    row_count, col_count = feats.shape
    slot_count = send_rows.shape[2]
    picked = feats[send_rows[0]]
    slot_live = jnp.arange(slot_count, dtype=jnp.int32)[None, :] < send_count[0][:, None]
    outgoing = jnp.where(slot_live[:, :, None], picked, jnp.zeros((), jnp.bfloat16))
    incoming = lax.all_to_all(outgoing, "parts", split_axis=0, concat_axis=0, tiled=True)
    halo_rows = incoming.reshape(-1, col_count)
    summed = jnp.dot(adj_local, feats, preferred_element_type=jnp.float32)
    summed = summed + jnp.dot(adj_halo, halo_rows, preferred_element_type=jnp.float32)
    convolved = summed.astype(jnp.bfloat16)
    out_cols = w_graph.shape[1]
    empty = jnp.zeros((row_count, out_cols), jnp.float32)
    weight_rows = w_graph
    projected = jnp.dot(
        lax.all_gather(convolved, "mp", axis=1, tiled=True),
        weight_rows,
        preferred_element_type=jnp.float32,
    )
    hidden = jax.nn.gelu(projected, approximate=False).astype(jnp.bfloat16)
    totals = (empty, empty, empty)
    portion = lax.all_gather(hidden, "mp", axis=1, tiled=True)
    outputs = []
    for running, weight in zip(totals, (w_query, w_key, w_value)):
        weight_rows = weight
        outputs.append(jnp.dot(portion, weight_rows, preferred_element_type=jnp.float32))
    queries, keys_raw, values_wide = tuple(outputs)
    live_mask = jnp.arange(row_count, dtype=jnp.int32)[:, None] < live[0]
    query_feat = jnp.where(live_mask, jax.nn.elu(queries) + 1.0, 0.0).astype(jnp.bfloat16)
    key_feat = jnp.where(live_mask, jax.nn.elu(keys_raw) + 1.0, 0.0).astype(jnp.bfloat16)
    values = values_wide.astype(jnp.bfloat16)
    key_values = lax.dot_general(
        key_feat,
        lax.all_gather(values, "mp", axis=1, tiled=True),
        (((0,), (0,)), ((), ())),
        preferred_element_type=jnp.float32,
    )
    query_wide = query_feat.astype(jnp.float32)
    key_wide = key_feat.astype(jnp.float32)
    key_total = jnp.sum(key_wide, axis=0)
    sq_pair = jnp.stack([jnp.sum(query_wide * query_wide), jnp.sum(key_wide * key_wide)])
    key_values, key_total, sq_pair = lax.psum((key_values, key_total, sq_pair), "parts")
    key_summary = key_values / math.sqrt(lax.axis_size("parts") * row_count)
    numer_part = jnp.dot(
        query_feat, key_values.astype(jnp.bfloat16), preferred_element_type=jnp.float32
    )
    denom_part = jnp.dot(query_wide, key_total, precision=lax.Precision.HIGHEST)
    numerator = lax.psum_scatter(
        numer_part.astype(jnp.bfloat16), "mp", scatter_dimension=1, tiled=True
    ).astype(jnp.float32)
    denominator, sq_pair = lax.psum((denom_part, sq_pair), "mp")
    inverse = lax.rsqrt(sq_pair[0]) * lax.rsqrt(sq_pair[1])
    result = (values.astype(jnp.float32) + numerator * inverse) / (1.0 + denominator * inverse)[
        :, None
    ]
    return (jnp.where(live_mask, result, 0.0), key_summary)


def dot(a, b):
    return jnp.dot(a, b, preferred_element_type=F32)


def kernel(
    n,
    chunks,
    feats_in,
    adj_local_in,
    adj_halo_in,
    send_rows_in,
    send_count_in,
    live,
    wg,
    wq,
    wk,
    wv,
    out,
    kv_out,
    feats,
    adj_local,
    adj_halo,
    send_rows,
    send_count,
    wbuf,
    outgoing,
    incoming,
    conv,
    hid,
    val,
    query,
    keyb,
    keyx,
    queryb,
    queryx,
    tbuf,
    ysend,
    yrecv,
    acc,
    zsend,
    zrecv,
    kvl,
    kvs,
    kvx,
    kvxs,
    nsend,
    nrecv,
    stat,
    den,
    isem,
    wsem,
    osem,
    feat_sem,
    halo_s,
    halo_r,
    fwd_s,
    fwd_r,
    hid_sem,
    key_s,
    key_r,
    query_s,
    query_r,
    val_sem,
    num_s,
    num_r,
    y_s,
    y_r,
    z_s,
    z_r,
    g_s,
    g_r,
    gy_s,
    gy_r,
    gx_s,
    gx_r,
    gc_s,
    gc_r,
    gd_s,
    gd_r,
    st_s,
    st_r,
    den_sem,
):
    p = lax.axis_index("parts")
    m = lax.axis_index("mp")
    c, y, z = p % 2, (p // 2) % 2, p // 4
    other = 1 - m
    sibling = p + 1 - 2 * c
    y_peer = p + 2 - 4 * y
    rows, cols = feats.shape[1:]
    slots = outgoing.shape[1]
    total = n * slots
    half, piece = cols // 2, zrecv.shape[2]
    quarter = 4 * piece

    z_near = z + 1 - 2 * (z % 2)
    z_far = lax.rem(z + 2, 4)
    z_mirror = 3 - z

    def spot_of(yy, zz):
        return pl.ds(pl.multiple_of((yy * 4 + zz) * piece, piece), piece)

    def make(src, dst, s_sem, r_sem, device):
        return pltpu.make_async_remote_copy(
            src_ref=src,
            dst_ref=dst,
            send_sem=s_sem,
            recv_sem=r_sem,
            device_id=device,
            device_id_type=MESH,
        )

    def send(src, dst, s_sem, r_sem, device):
        copy = make(src, dst, s_sem, r_sem, device)
        copy.start()
        return copy

    def wait_for(like, sem):
        pltpu.make_async_copy(like, like, sem).wait()

    inputs = []
    for i, (source, place) in enumerate(
        (
            (send_rows_in, send_rows),
            (send_count_in, send_count),
            (feats_in, feats.at[m]),
            (adj_local_in, adj_local),
            (adj_halo_in, adj_halo),
        )
    ):
        load = pltpu.make_async_copy(source, place, isem.at[i])
        load.start()
        inputs.append(load)
    loads = []
    for i, w in enumerate((wg, wk, wv, wq)):
        load = pltpu.make_async_copy(w, wbuf.at[i], wsem.at[i])
        load.start()
        loads.append(load)

    barrier = pltpu.get_barrier_semaphore()
    for d in range(1, n):
        pl.semaphore_signal(
            barrier, inc=1, device_id={"parts": lax.rem(p + d, n)}, device_id_type=MESH
        )
    for to in (p, sibling, y_peer):
        pl.semaphore_signal(
            barrier, inc=1, device_id={"parts": to, "mp": other}, device_id_type=MESH
        )

    for load in inputs:
        load.wait()

    owner = lax.broadcasted_iota(jnp.int32, (total, n), 0) // slots
    is_owner = owner == lax.broadcasted_iota(jnp.int32, (total, n), 1)
    spot = lax.broadcasted_iota(jnp.int32, (total, slots), 0) % slots
    is_spot = spot == lax.broadcasted_iota(jnp.int32, (total, slots), 1)
    spread = lax.dot_general(
        is_owner.astype(F32),
        send_rows[...].astype(F32),
        (((1,), (1,)), ((), ())),
        precision=lax.Precision.HIGHEST,
        preferred_element_type=F32,
    )
    index = jnp.sum(jnp.where(is_spot, spread, 0.0), axis=1, keepdims=True)
    count = jnp.sum(
        jnp.where(is_owner, send_count[...].astype(F32), 0.0), axis=1, keepdims=True
    )
    slot_id = jnp.sum(
        jnp.where(is_spot, lax.broadcasted_iota(jnp.int32, (total, slots), 1), 0).astype(F32),
        axis=1,
        keepdims=True,
    )
    index = jnp.where(slot_id < count, index, -1.0)
    node = lax.broadcasted_iota(jnp.int32, (total, rows), 1).astype(F32)
    pick = jnp.where(index == node, 1.0, 0.0).astype(BF16)
    outgoing[...] = dot(pick, feats[m]).reshape(n, slots, cols).astype(BF16)

    def partner(k):
        kz, ky, kc = k // 4, (k // 2) % 2, k % 2
        zz = (z, z_near, z_far, z_mirror)[kz]
        yy = 1 - y if ky else y
        cc = 1 - c if kc else c
        return zz * 4 + yy * 2 + cc

    pl.semaphore_wait(barrier, n + 2)
    for k in (*range(12, n), *range(8, 12), *range(4, 8), *range(1, 4)):
        to = partner(k)
        send(outgoing.at[to], incoming.at[m, p], halo_s, halo_r.at[k // 4], {"parts": to})
    swap_feats = send(feats.at[m], feats.at[m], feat_sem.at[0], feat_sem.at[1], {"mp": other})
    send(outgoing.at[p], incoming.at[m, p], fwd_s, fwd_r, {"mp": other})
    incoming[m, p] = outgoing[p]
    local_mine = dot(adj_local[...], feats[m])
    for kz in range(4):
        members = range(max(1, 4 * kz), 4 * kz + 4)
        wait_for(outgoing.at[pl.ds(0, len(members))], halo_r.at[kz])
        for k in members:
            block = incoming.at[m, partner(k)]
            send(block, block, fwd_s, fwd_r, {"mp": other})

    def convolve(side, local_sum):
        arrived = incoming[side].astype(F32).reshape(total, cols).astype(BF16)
        conv[side] = (local_sum + dot(adj_halo[...], arrived)).astype(BF16)

    mine = pl.ds(pl.multiple_of(m * cols, cols), cols)
    theirs = pl.ds(pl.multiple_of(other * cols, cols), cols)
    convolve(m, local_mine)
    loads[0].wait()
    projected = dot(conv[m], wbuf[0, mine, :])
    swap_feats.wait_recv()
    local_theirs = dot(adj_local[...], feats[other])
    wait_for(outgoing, fwd_r)
    convolve(other, local_theirs)
    projected = projected + dot(conv[other], wbuf[0, theirs, :])
    hid[m] = (0.5 * projected * (1.0 + lax.erf(projected * math.sqrt(0.5)))).astype(BF16)
    swap = send(hid.at[m], hid.at[m], hid_sem.at[0], hid_sem.at[1], {"mp": other})
    for load in loads[1:]:
        load.wait()
    own = hid[m]
    raw_k = dot(own, wbuf[1, mine, :])
    raw_v = dot(own, wbuf[2, mine, :])
    raw_q = dot(own, wbuf[3, mine, :])
    live_mask = lax.broadcasted_iota(jnp.int32, (rows, 1), 0) < live[0]

    def feature(x):
        x = jnp.where(x > 0.0, x + 1.0, jnp.exp(jnp.minimum(x, 0.0)))
        return jnp.where(live_mask, x, 0.0).astype(BF16)

    def spread_blocks(blocks, place, s_sems, r_sems):
        away = blocks.at[1 - c]
        return [
            send(blocks.at[c], place.at[1, c], s_sems.at[0], r_sems.at[0], {"mp": other}),
            send(
                away,
                place.at[1, c],
                s_sems.at[1],
                r_sems.at[1],
                {"parts": sibling, "mp": other},
            ),
            send(away, place.at[0, c], s_sems.at[2], r_sems.at[2], {"parts": sibling}),
        ]

    swap.wait_recv()
    rest = hid[other]
    key_feat = feature(raw_k + dot(rest, wbuf[1, theirs, :]))
    key_wide = key_feat.astype(F32)
    key_t = key_wide.T.astype(BF16)
    for b in range(2):
        keyb[b] = key_t[b * half : (b + 1) * half]
    keys = spread_blocks(keyb, keyx, key_s, key_r)
    val[c] = (raw_v + dot(rest, wbuf[2, theirs, :])).astype(BF16)
    values = send(val.at[c], val.at[c], val_sem.at[0], val_sem.at[1], {"parts": sibling})
    query_feat = feature(raw_q + dot(rest, wbuf[3, theirs, :]))
    query[...] = query_feat
    for b in range(2):
        queryb[b] = query_feat[:, b * half : (b + 1) * half]
    query_wide = query_feat.astype(F32)
    lane = lax.broadcasted_iota(jnp.int32, (1, 128), 1)
    query_sq = jnp.sum(jnp.sum(query_wide * query_wide, axis=0, keepdims=True), axis=1, keepdims=True)
    key_sq = jnp.sum(jnp.sum(key_wide * key_wide, axis=0, keepdims=True), axis=1, keepdims=True)
    stat[0, :, :cols] = jnp.sum(key_wide, axis=0, keepdims=True)
    stat[0, :, cols:] = jnp.where(lane == 0, query_sq, jnp.where(lane == 1, key_sq, 0.0))
    for k in range(1, n):
        send(stat.at[0], stat.at[k], st_s, st_r, {"parts": partner(k)})
    queries = spread_blocks(queryb, queryx, query_s, query_r)

    y_copies, g_copies, num_copies, numer = {}, {}, {}, {}
    others = (z_near, z_far, z_mirror)

    def span(i):
        return pl.ds(chunks[i][1], chunks[i][2])

    def product(i):
        a, columns = chunks[i][0], span(i)
        if a == 0:
            first, second = keyb[c], keyx[0, 1 - c]
        else:
            first, second = keyx[1, c], keyx[1, 1 - c]
        whole = dot(first, val[c, :, columns]) + dot(second, val[1 - c, :, columns])
        tbuf[a, :, :, columns] = whole.reshape(2, quarter, chunks[i][2])
        ysend[a, :, columns] = tbuf[a, 1 - y, :, columns].astype(BF16)
        y_copies[i] = send(
            ysend.at[a, :, columns], yrecv.at[a, :, columns], y_s, y_r.at[i], {"parts": y_peer}
        )

    def on_z(zz):
        return {"parts": zz * 4 + p % 4}

    def z_send(i):
        a, columns = chunks[i][0], span(i)
        y_copies[i].wait_recv()
        whole = tbuf[a, y, :, columns] + yrecv[a, :, columns].astype(F32)
        acc[a, :, :, columns] = whole.reshape(4, piece, chunks[i][2])
        zsend[a, :, :, columns] = acc[a, :, :, columns].astype(BF16)
        for k in (2, 1, 0):
            send(
                zsend.at[a, others[k], :, columns],
                zrecv.at[a, k, :, columns],
                z_s,
                z_r.at[i],
                on_z(others[k]),
            )

    def pass_on(i, zz, direct):
        a, columns = chunks[i][0], span(i)
        place = kvl.at[a, spot_of(y, zz), columns]
        send(place, place, gy_s, gy_r.at[i], {"parts": y_peer})
        if a == 1:
            target = kvx.at[spot_of(y, zz), columns]
            send(place, target, gx_s, gx_r.at[i], {"mp": other})
            if direct:
                send(place, target, gx_s, gx_r.at[i], {"parts": y_peer, "mp": other})

    def z_final(i):
        a, columns = chunks[i][0], span(i)
        wait_for(zrecv.at[a, :, :, columns], z_r.at[i])
        final = acc[a, z, :, columns]
        for k in range(3):
            final = final + zrecv[a, k, :, columns].astype(F32)
        place = kvl.at[a, spot_of(y, z), columns]
        place[...] = final.astype(BF16)
        g_copies[i] = [
            send(place, place, g_s, g_r.at[i, k], on_z(others[k])) for k in (2, 1, 0)
        ]
        pass_on(i, z, True)

    def z_gather(i):
        for k in range(3):
            g_copies[i][2 - k].wait_recv()
            pass_on(i, others[k], k == 0)

    def store(place, core, side, columns):
        target = kv_out.at[
            pl.ds(pl.multiple_of(core * half, half), half),
            pl.ds(pl.multiple_of(side * cols + columns.start, 128), columns.size),
        ]
        pltpu.make_async_copy(place, target, osem).start()

    def y_gather(i):
        a, columns = chunks[i][0], span(i)
        wait_for(yrecv.at[a, :, columns], gy_r.at[i])
        if a == 0:
            send(
                kvl.at[0, :, columns], kvs.at[:, columns], gc_s, gc_r.at[i], {"parts": sibling}
            )
            return
        for zz in others[1:]:
            part = spot_of(1 - y, zz)
            send(
                kvl.at[1, part, columns],
                kvx.at[part, columns],
                gx_s,
                gx_r.at[i],
                {"mp": other},
            )
        mine, theirs = kvl[0, :, columns], kvl[1, :, columns]
        nsend[:, columns] = dot(queryx[0, 1 - c], mine) + dot(queryx[1, 1 - c], theirs)
        num_copies[i] = send(
            nsend.at[:, columns], nrecv.at[:, columns], num_s, num_r.at[i], {"parts": sibling}
        )
        numer[i] = dot(queryb[c], mine) + dot(queryx[1, c], theirs)

    def denominators():
        wait_for(stat.at[pl.ds(1, n - 1)], st_r)
        sums = stat[0]
        for k in range(1, n):
            sums = sums + stat[k]
        den[m, :rows, :] = jnp.broadcast_to(
            jnp.sum(query[...].astype(F32) * sums[:, :cols], axis=1, keepdims=True),
            (rows, 128),
        )
        den[m, rows:, :] = jnp.broadcast_to(sums[:, cols:], (8, 128))
        return send(den.at[m], den.at[m], den_sem.at[0], den_sem.at[1], {"mp": other})

    keys[2].wait_recv()
    values.wait_recv()
    early = [i for i, chunk in enumerate(chunks) if chunk[0] == 0]
    for i in early:
        product(i)
    for copy in keys[:2]:
        copy.wait_recv()
    for i in range(len(chunks)):
        if i not in early:
            product(i)

    for i in range(len(chunks)):
        z_send(i)
    den_swap = denominators()
    for step in (z_final, z_gather):
        for i in range(len(chunks)):
            step(i)
    for copy in queries:
        copy.wait_recv()
    for i in range(len(chunks)):
        y_gather(i)

    den_swap.wait_recv()
    square = den[0, rows : rows + 1, :] + den[1, rows : rows + 1, :]
    query_sq = jnp.sum(jnp.where(lane == 0, square, 0.0), axis=1, keepdims=True)
    key_sq = jnp.sum(jnp.where(lane == 1, square, 0.0), axis=1, keepdims=True)
    inverse = lax.rsqrt(query_sq) * lax.rsqrt(key_sq)
    denominator = den[0, :rows, 0:1] + den[1, :rows, 0:1]
    scale = 1.0 + denominator * inverse

    late = [i for i in range(len(chunks)) if i not in early]
    for i in early:
        store(kvl.at[0, :, span(i)], c, m, span(i))
    for i in early:
        wait_for(kvs.at[:, span(i)], gc_r.at[i])
        store(kvs.at[:, span(i)], 1 - c, m, span(i))
    for i in late:
        columns = span(i)
        num_copies[i].wait_recv()
        result = val[c, :, columns].astype(F32) + (numer[i] + nrecv[:, columns]) * inverse
        out[:, columns] = jnp.where(live_mask, result / scale, 0.0)
    last = {}
    for i in late:
        place = kvx.at[:, span(i)]
        wait_for(place, gx_r.at[i])
        last[i] = send(place, kvxs.at[:, span(i)], gd_s, gd_r.at[i], {"parts": sibling})
        store(place, c, other, span(i))
    for i in late:
        last[i].wait_recv()
        store(kvxs.at[:, span(i)], 1 - c, other, span(i))

    wait_for(outgoing.at[pl.ds(0, n - 1)], halo_s)
    wait_for(outgoing, fwd_s)
    wait_for(stat.at[pl.ds(1, n - 1)], st_s)
    wait_for(ysend, y_s)
    wait_for(zrecv, z_s)
    wait_for(zrecv, g_s)
    wait_for(yrecv, gy_s)
    wait_for(kvx, gx_s)
    wait_for(kvs, gc_s)
    wait_for(kvx, gd_s)
    wait_for(nsend, num_s)
    for copy in (swap_feats, swap, *keys, values, *queries, den_swap):
        copy.wait_send()
    wait_for(kv_out, osem)


def fused(
    feats, adj_local, adj_halo, w_graph, w_query, w_key, w_value, send_rows, send_count, live
):
    n = lax.axis_size("parts")
    rows, cols = feats.shape
    slots = send_rows.shape[2]
    depth = w_graph.shape[0]
    half, piece = cols // 2, cols // 16
    quarter = half // 2
    chunks = ((0, 0, half), (0, half, half), (1, 0, half), (1, half, quarter), (1, half + quarter, quarter))
    count = len(chunks)
    vmem = pl.BlockSpec(memory_space=pltpu.VMEM)
    hbm = pl.BlockSpec(memory_space=pltpu.HBM)
    dma = pltpu.SemaphoreType.DMA
    place = functools.partial(pltpu.with_memory_space_constraint, memory_space=pltpu.HBM)
    out, kv = pl.pallas_call(
        functools.partial(kernel, n, chunks),
        out_shape=(
            jax.ShapeDtypeStruct((rows, cols), F32),
            jax.ShapeDtypeStruct((cols, depth), BF16),
        ),
        in_specs=[hbm] * 5 + [pl.BlockSpec(memory_space=pltpu.SMEM)] + [hbm] * 4,
        out_specs=(vmem, pl.BlockSpec(memory_space=pl.ANY)),
        scratch_shapes=[
            pltpu.VMEM((2, rows, cols), BF16),
            pltpu.VMEM(adj_local.shape, BF16),
            pltpu.VMEM(adj_halo.shape, BF16),
            pltpu.VMEM((slots, n), jnp.int32),
            pltpu.VMEM((1, n), jnp.int32),
            pltpu.VMEM((4, depth, cols), BF16),
            pltpu.VMEM((n, slots, cols), BF16),
            pltpu.VMEM((2, n, slots, cols), BF16),
            pltpu.VMEM((2, rows, cols), BF16),
            pltpu.VMEM((2, rows, cols), BF16),
            pltpu.VMEM((2, rows, cols), BF16),
            pltpu.VMEM((rows, cols), BF16),
            pltpu.VMEM((2, half, rows), BF16),
            pltpu.VMEM((2, 2, half, rows), BF16),
            pltpu.VMEM((2, rows, half), BF16),
            pltpu.VMEM((2, 2, rows, half), BF16),
            pltpu.VMEM((2, 2, 4 * piece, cols), F32),
            pltpu.VMEM((2, 4 * piece, cols), BF16),
            pltpu.VMEM((2, 4 * piece, cols), BF16),
            pltpu.VMEM((2, 4, piece, cols), F32),
            pltpu.VMEM((2, 4, piece, cols), BF16),
            pltpu.VMEM((2, 3, piece, cols), BF16),
            pltpu.VMEM((2, half, cols), BF16),
            pltpu.VMEM((half, cols), BF16),
            pltpu.VMEM((half, cols), BF16),
            pltpu.VMEM((half, cols), BF16),
            pltpu.VMEM((rows, cols), F32),
            pltpu.VMEM((rows, cols), F32),
            pltpu.VMEM((n, 1, cols + 128), F32),
            pltpu.VMEM((2, rows + 8, 128), F32),
            dma((5,)),
            dma((4,)),
            dma,
            dma((2,)),
            dma,
            dma((4,)),
            dma,
            dma,
            dma((2,)),
            dma((3,)),
            dma((3,)),
            dma((3,)),
            dma((3,)),
            dma((2,)),
            dma,
            dma((count,)),
            dma,
            dma((count,)),
            dma,
            dma((count,)),
            dma,
            dma((count, 3)),
            dma,
            dma((count,)),
            dma,
            dma((count,)),
            dma,
            dma((count,)),
            dma,
            dma((count,)),
            dma,
            dma,
            dma((2,)),
        ],
        compiler_params=pltpu.CompilerParams(
            collective_id=0, has_side_effects=True, vmem_limit_bytes=24 * 1024 * 1024
        ),
    )(
        *(place(a) for a in (feats, adj_local, adj_halo, send_rows[0].T, send_count)),
        live,
        *(place(w) for w in (w_graph, w_query, w_key, w_value)),
    )
    return out, kv.astype(F32) / math.sqrt(n * rows)


def local(*args):
    n = lax.axis_size("parts")
    rows, cols = args[0].shape
    slots = args[7].shape[2]
    fits = (
        lax.axis_size("mp") == 2
        and n == 16
        and cols % 512 == 0
        and rows % 128 == 0
        and (n * slots) % 16 == 0
        and slots % 8 == 0
    )
    return fused(*args) if fits else plain(*args)


def solution(mesh):
    return jax.shard_map(
        local,
        mesh=mesh,
        in_specs=(
            P("parts", "mp"),
            P("parts", None),
            P("parts", None),
            P(None, "mp"),
            P(None, "mp"),
            P(None, "mp"),
            P(None, "mp"),
            P("parts", None, None),
            P("parts", None),
            P("parts"),
        ),
        out_specs=(P("parts", "mp"), P("mp", None)),
        check_vma=False,
    )
```

```python
import functools
import math

import jax
import jax.numpy as jnp
from jax import lax
from jax.experimental import pallas as pl
from jax.experimental.pallas import tpu as pltpu
from jax.sharding import PartitionSpec as P

MESH = pl.DeviceIdType.MESH
F32 = jnp.float32
BF16 = jnp.bfloat16


def plain(
    feats, adj_local, adj_halo, w_graph, w_query, w_key, w_value, send_rows, send_count, live
):
    row_count, col_count = feats.shape
    slot_count = send_rows.shape[2]
    picked = feats[send_rows[0]]
    slot_live = jnp.arange(slot_count, dtype=jnp.int32)[None, :] < send_count[0][:, None]
    outgoing = jnp.where(slot_live[:, :, None], picked, jnp.zeros((), jnp.bfloat16))
    incoming = lax.all_to_all(outgoing, "parts", split_axis=0, concat_axis=0, tiled=True)
    halo_rows = incoming.reshape(-1, col_count)
    summed = jnp.dot(adj_local, feats, preferred_element_type=jnp.float32)
    summed = summed + jnp.dot(adj_halo, halo_rows, preferred_element_type=jnp.float32)
    convolved = summed.astype(jnp.bfloat16)
    out_cols = w_graph.shape[1]
    empty = jnp.zeros((row_count, out_cols), jnp.float32)
    weight_rows = w_graph
    projected = jnp.dot(
        lax.all_gather(convolved, "mp", axis=1, tiled=True),
        weight_rows,
        preferred_element_type=jnp.float32,
    )
    hidden = jax.nn.gelu(projected, approximate=False).astype(jnp.bfloat16)
    totals = (empty, empty, empty)
    portion = lax.all_gather(hidden, "mp", axis=1, tiled=True)
    outputs = []
    for running, weight in zip(totals, (w_query, w_key, w_value)):
        weight_rows = weight
        outputs.append(jnp.dot(portion, weight_rows, preferred_element_type=jnp.float32))
    queries, keys_raw, values_wide = tuple(outputs)
    live_mask = jnp.arange(row_count, dtype=jnp.int32)[:, None] < live[0]
    query_feat = jnp.where(live_mask, jax.nn.elu(queries) + 1.0, 0.0).astype(jnp.bfloat16)
    key_feat = jnp.where(live_mask, jax.nn.elu(keys_raw) + 1.0, 0.0).astype(jnp.bfloat16)
    values = values_wide.astype(jnp.bfloat16)
    key_values = lax.dot_general(
        key_feat,
        lax.all_gather(values, "mp", axis=1, tiled=True),
        (((0,), (0,)), ((), ())),
        preferred_element_type=jnp.float32,
    )
    query_wide = query_feat.astype(jnp.float32)
    key_wide = key_feat.astype(jnp.float32)
    key_total = jnp.sum(key_wide, axis=0)
    sq_pair = jnp.stack([jnp.sum(query_wide * query_wide), jnp.sum(key_wide * key_wide)])
    key_values, key_total, sq_pair = lax.psum((key_values, key_total, sq_pair), "parts")
    key_summary = key_values / math.sqrt(lax.axis_size("parts") * row_count)
    numer_part = jnp.dot(
        query_feat, key_values.astype(jnp.bfloat16), preferred_element_type=jnp.float32
    )
    denom_part = jnp.dot(query_wide, key_total, precision=lax.Precision.HIGHEST)
    numerator = lax.psum_scatter(
        numer_part.astype(jnp.bfloat16), "mp", scatter_dimension=1, tiled=True
    ).astype(jnp.float32)
    denominator, sq_pair = lax.psum((denom_part, sq_pair), "mp")
    inverse = lax.rsqrt(sq_pair[0]) * lax.rsqrt(sq_pair[1])
    result = (values.astype(jnp.float32) + numerator * inverse) / (1.0 + denominator * inverse)[
        :, None
    ]
    return (jnp.where(live_mask, result, 0.0), key_summary)


def dot(a, b):
    return jnp.dot(a, b, preferred_element_type=F32)


def kernel(
    n,
    chunks,
    feats_in,
    adj_local_in,
    adj_halo_in,
    send_rows_in,
    send_count_in,
    live,
    wg,
    wq,
    wk,
    wv,
    out,
    kv_out,
    feats,
    adj_local,
    adj_halo,
    send_rows,
    send_count,
    wbuf,
    outgoing,
    incoming,
    conv,
    hid,
    val,
    query,
    keyb,
    keyx,
    queryb,
    queryx,
    tbuf,
    ysend,
    yrecv,
    acc,
    zsend,
    zrecv,
    kvl,
    kvs,
    kvx,
    kvxs,
    nsend,
    nrecv,
    stat,
    den,
    isem,
    wsem,
    osem,
    feat_sem,
    halo_s,
    halo_r,
    fwd_s,
    fwd_r,
    hid_sem,
    key_s,
    key_r,
    query_s,
    query_r,
    val_sem,
    num_s,
    num_r,
    y_s,
    y_r,
    z_s,
    z_r,
    g_s,
    g_r,
    gy_s,
    gy_r,
    gx_s,
    gx_r,
    gc_s,
    gc_r,
    gd_s,
    gd_r,
    st_s,
    st_r,
    den_sem,
):
    p = lax.axis_index("parts")
    m = lax.axis_index("mp")
    c, y, z = p % 2, (p // 2) % 2, p // 4
    other = 1 - m
    sibling = p + 1 - 2 * c
    y_peer = p + 2 - 4 * y
    rows, cols = feats.shape[1:]
    slots = outgoing.shape[1]
    total = n * slots
    half, piece = cols // 2, zrecv.shape[2]
    quarter = 4 * piece

    z_near = z + 1 - 2 * (z % 2)
    z_far = lax.rem(z + 2, 4)
    z_mirror = 3 - z

    def spot_of(yy, zz):
        return pl.ds(pl.multiple_of((yy * 4 + zz) * piece, piece), piece)

    def make(src, dst, s_sem, r_sem, device):
        return pltpu.make_async_remote_copy(
            src_ref=src,
            dst_ref=dst,
            send_sem=s_sem,
            recv_sem=r_sem,
            device_id=device,
            device_id_type=MESH,
        )

    def send(src, dst, s_sem, r_sem, device):
        copy = make(src, dst, s_sem, r_sem, device)
        copy.start()
        return copy

    def wait_for(like, sem):
        pltpu.make_async_copy(like, like, sem).wait()

    inputs = []
    for i, (source, place) in enumerate(
        (
            (send_rows_in, send_rows),
            (send_count_in, send_count),
            (feats_in, feats.at[m]),
            (adj_local_in, adj_local),
            (adj_halo_in, adj_halo),
        )
    ):
        load = pltpu.make_async_copy(source, place, isem.at[i])
        load.start()
        inputs.append(load)

    barrier = pltpu.get_barrier_semaphore()
    for d in range(1, n):
        pl.semaphore_signal(
            barrier, inc=1, device_id={"parts": lax.rem(p + d, n)}, device_id_type=MESH
        )
    for to in (p, sibling, y_peer):
        pl.semaphore_signal(
            barrier, inc=1, device_id={"parts": to, "mp": other}, device_id_type=MESH
        )

    for load in inputs:
        load.wait()
    loads = []
    for i, w in enumerate((wg, wk, wv, wq)):
        load = pltpu.make_async_copy(w, wbuf.at[i], wsem.at[i])
        load.start()
        loads.append(load)

    owner = lax.broadcasted_iota(jnp.int32, (total, n), 0) // slots
    is_owner = owner == lax.broadcasted_iota(jnp.int32, (total, n), 1)
    spot = lax.broadcasted_iota(jnp.int32, (total, slots), 0) % slots
    is_spot = spot == lax.broadcasted_iota(jnp.int32, (total, slots), 1)
    spread = lax.dot_general(
        is_owner.astype(F32),
        send_rows[...].astype(F32),
        (((1,), (1,)), ((), ())),
        precision=lax.Precision.HIGHEST,
        preferred_element_type=F32,
    )
    index = jnp.sum(jnp.where(is_spot, spread, 0.0), axis=1, keepdims=True)
    count = jnp.sum(
        jnp.where(is_owner, send_count[...].astype(F32), 0.0), axis=1, keepdims=True
    )
    slot_id = jnp.sum(
        jnp.where(is_spot, lax.broadcasted_iota(jnp.int32, (total, slots), 1), 0).astype(F32),
        axis=1,
        keepdims=True,
    )
    index = jnp.where(slot_id < count, index, -1.0)
    node = lax.broadcasted_iota(jnp.int32, (total, rows), 1).astype(F32)
    pick = jnp.where(index == node, 1.0, 0.0).astype(BF16)
    outgoing[...] = dot(pick, feats[m]).reshape(n, slots, cols).astype(BF16)

    def partner(k):
        kz, ky, kc = k // 4, (k // 2) % 2, k % 2
        zz = (z, z_near, z_far, z_mirror)[kz]
        yy = 1 - y if ky else y
        cc = 1 - c if kc else c
        return zz * 4 + yy * 2 + cc

    pl.semaphore_wait(barrier, n + 2)
    for k in (*range(12, n), *range(8, 12), *range(4, 8), *range(1, 4)):
        to = partner(k)
        send(outgoing.at[to], incoming.at[m, p], halo_s, halo_r.at[k // 4], {"parts": to})
    swap_feats = send(feats.at[m], feats.at[m], feat_sem.at[0], feat_sem.at[1], {"mp": other})
    incoming[m, p] = outgoing[p]
    local_mine = dot(adj_local[...], feats[m])
    for kz in range(4):
        members = range(max(1, 4 * kz), 4 * kz + 4)
        wait_for(outgoing.at[pl.ds(0, len(members))], halo_r.at[kz])
        first = pl.multiple_of((z, z_near, z_far, z_mirror)[kz] * 4, 4)
        block = incoming.at[m, pl.ds(first, 4)]
        send(block, block, fwd_s, fwd_r, {"mp": other})

    def convolve(side, local_sum):
        arrived = incoming[side].astype(F32).reshape(total, cols).astype(BF16)
        conv[side] = (local_sum + dot(adj_halo[...], arrived)).astype(BF16)

    mine = pl.ds(pl.multiple_of(m * cols, cols), cols)
    theirs = pl.ds(pl.multiple_of(other * cols, cols), cols)
    convolve(m, local_mine)
    loads[0].wait()
    projected = dot(conv[m], wbuf[0, mine, :])
    swap_feats.wait_recv()
    local_theirs = dot(adj_local[...], feats[other])
    wait_for(outgoing, fwd_r)
    convolve(other, local_theirs)
    projected = projected + dot(conv[other], wbuf[0, theirs, :])
    hid[m] = (0.5 * projected * (1.0 + lax.erf(projected * math.sqrt(0.5)))).astype(BF16)
    swap = send(hid.at[m], hid.at[m], hid_sem.at[0], hid_sem.at[1], {"mp": other})
    for load in loads[1:]:
        load.wait()
    own = hid[m]
    raw_k = dot(own, wbuf[1, mine, :])
    raw_v = dot(own, wbuf[2, mine, :])
    raw_q = dot(own, wbuf[3, mine, :])
    live_mask = lax.broadcasted_iota(jnp.int32, (rows, 1), 0) < live[0]

    def feature(x):
        x = jnp.where(x > 0.0, x + 1.0, jnp.exp(jnp.minimum(x, 0.0)))
        return jnp.where(live_mask, x, 0.0).astype(BF16)

    def spread_blocks(blocks, place, s_sems, r_sems):
        away = blocks.at[1 - c]
        return [
            send(blocks.at[c], place.at[1, c], s_sems.at[0], r_sems.at[0], {"mp": other}),
            send(
                away,
                place.at[1, c],
                s_sems.at[1],
                r_sems.at[1],
                {"parts": sibling, "mp": other},
            ),
            send(away, place.at[0, c], s_sems.at[2], r_sems.at[2], {"parts": sibling}),
        ]

    swap.wait_recv()
    rest = hid[other]
    key_feat = feature(raw_k + dot(rest, wbuf[1, theirs, :]))
    key_wide = key_feat.astype(F32)
    key_t = key_wide.T.astype(BF16)
    for b in range(2):
        keyb[b] = key_t[b * half : (b + 1) * half]
    keys = spread_blocks(keyb, keyx, key_s, key_r)
    val[c] = (raw_v + dot(rest, wbuf[2, theirs, :])).astype(BF16)
    values = send(val.at[c], val.at[c], val_sem.at[0], val_sem.at[1], {"parts": sibling})
    query_feat = feature(raw_q + dot(rest, wbuf[3, theirs, :]))
    query[...] = query_feat
    for b in range(2):
        queryb[b] = query_feat[:, b * half : (b + 1) * half]
    query_wide = query_feat.astype(F32)
    lane = lax.broadcasted_iota(jnp.int32, (1, 128), 1)
    query_sq = jnp.sum(jnp.sum(query_wide * query_wide, axis=0, keepdims=True), axis=1, keepdims=True)
    key_sq = jnp.sum(jnp.sum(key_wide * key_wide, axis=0, keepdims=True), axis=1, keepdims=True)
    stat[0, :, :cols] = jnp.sum(key_wide, axis=0, keepdims=True)
    stat[0, :, cols:] = jnp.where(lane == 0, query_sq, jnp.where(lane == 1, key_sq, 0.0))
    for k in range(1, n):
        send(stat.at[0], stat.at[k], st_s, st_r, {"parts": partner(k)})
    queries = spread_blocks(queryb, queryx, query_s, query_r)

    y_copies, g_copies, num_copies, numer = {}, {}, {}, {}
    others = (z_near, z_far, z_mirror)

    def span(i):
        return pl.ds(chunks[i][1], chunks[i][2])

    def product(i):
        a, columns = chunks[i][0], span(i)
        if a == 0:
            first, second = keyb[c], keyx[0, 1 - c]
        else:
            first, second = keyx[1, c], keyx[1, 1 - c]
        whole = dot(first, val[c, :, columns]) + dot(second, val[1 - c, :, columns])
        tbuf[a, :, :, columns] = whole.reshape(2, quarter, chunks[i][2])
        ysend[a, :, columns] = tbuf[a, 1 - y, :, columns].astype(BF16)
        y_copies[i] = send(
            ysend.at[a, :, columns], yrecv.at[a, :, columns], y_s, y_r.at[i], {"parts": y_peer}
        )

    def on_z(zz):
        return {"parts": zz * 4 + p % 4}

    def z_send(i):
        a, columns = chunks[i][0], span(i)
        y_copies[i].wait_recv()
        whole = tbuf[a, y, :, columns] + yrecv[a, :, columns].astype(F32)
        acc[a, :, :, columns] = whole.reshape(4, piece, chunks[i][2])
        zsend[a, :, :, columns] = acc[a, :, :, columns].astype(BF16)
        for k in (2, 1, 0):
            send(
                zsend.at[a, others[k], :, columns],
                zrecv.at[a, k, :, columns],
                z_s,
                z_r.at[i],
                on_z(others[k]),
            )

    def pass_on(i, zz, direct):
        a, columns = chunks[i][0], span(i)
        place = kvl.at[a, spot_of(y, zz), columns]
        send(place, place, gy_s, gy_r.at[i], {"parts": y_peer})
        if a == 1:
            target = kvx.at[spot_of(y, zz), columns]
            send(place, target, gx_s, gx_r.at[i], {"mp": other})
            if direct:
                send(place, target, gx_s, gx_r.at[i], {"parts": y_peer, "mp": other})

    def z_final(i):
        a, columns = chunks[i][0], span(i)
        wait_for(zrecv.at[a, :, :, columns], z_r.at[i])
        final = acc[a, z, :, columns]
        for k in range(3):
            final = final + zrecv[a, k, :, columns].astype(F32)
        place = kvl.at[a, spot_of(y, z), columns]
        place[...] = final.astype(BF16)
        g_copies[i] = [
            send(place, place, g_s, g_r.at[i, k], on_z(others[k])) for k in (2, 1, 0)
        ]
        pass_on(i, z, True)

    def z_gather(i):
        for k in range(3):
            g_copies[i][2 - k].wait_recv()
            pass_on(i, others[k], k == 0)

    def store(place, core, side, columns):
        target = kv_out.at[
            pl.ds(pl.multiple_of(core * half, half), half),
            pl.ds(pl.multiple_of(side * cols + columns.start, 128), columns.size),
        ]
        pltpu.make_async_copy(place, target, osem).start()

    def y_gather(i):
        a, columns = chunks[i][0], span(i)
        wait_for(yrecv.at[a, :, columns], gy_r.at[i])
        if a == 0:
            send(
                kvl.at[0, :, columns], kvs.at[:, columns], gc_s, gc_r.at[i], {"parts": sibling}
            )
            return
        for zz in others[1:]:
            part = spot_of(1 - y, zz)
            send(
                kvl.at[1, part, columns],
                kvx.at[part, columns],
                gx_s,
                gx_r.at[i],
                {"mp": other},
            )
        mine, theirs = kvl[0, :, columns], kvl[1, :, columns]
        nsend[:, columns] = dot(queryx[0, 1 - c], mine) + dot(queryx[1, 1 - c], theirs)
        num_copies[i] = send(
            nsend.at[:, columns], nrecv.at[:, columns], num_s, num_r.at[i], {"parts": sibling}
        )
        numer[i] = dot(queryb[c], mine) + dot(queryx[1, c], theirs)

    def denominators():
        wait_for(stat.at[pl.ds(1, n - 1)], st_r)
        sums = stat[0]
        for k in range(1, n):
            sums = sums + stat[k]
        den[m, :rows, :] = jnp.broadcast_to(
            jnp.sum(query[...].astype(F32) * sums[:, :cols], axis=1, keepdims=True),
            (rows, 128),
        )
        den[m, rows:, :] = jnp.broadcast_to(sums[:, cols:], (8, 128))
        return send(den.at[m], den.at[m], den_sem.at[0], den_sem.at[1], {"mp": other})

    keys[2].wait_recv()
    values.wait_recv()
    early = [i for i, chunk in enumerate(chunks) if chunk[0] == 0]
    for i in early:
        product(i)
    for copy in keys[:2]:
        copy.wait_recv()
    for i in range(len(chunks)):
        if i not in early:
            product(i)

    for i in range(len(chunks)):
        z_send(i)
    den_swap = denominators()
    for step in (z_final, z_gather):
        for i in range(len(chunks)):
            step(i)
    for copy in queries:
        copy.wait_recv()
    for i in range(len(chunks)):
        y_gather(i)

    den_swap.wait_recv()
    square = den[0, rows : rows + 1, :] + den[1, rows : rows + 1, :]
    query_sq = jnp.sum(jnp.where(lane == 0, square, 0.0), axis=1, keepdims=True)
    key_sq = jnp.sum(jnp.where(lane == 1, square, 0.0), axis=1, keepdims=True)
    inverse = lax.rsqrt(query_sq) * lax.rsqrt(key_sq)
    denominator = den[0, :rows, 0:1] + den[1, :rows, 0:1]
    scale = 1.0 + denominator * inverse

    late = [i for i in range(len(chunks)) if i not in early]
    for i in early:
        store(kvl.at[0, :, span(i)], c, m, span(i))
    for i in early:
        wait_for(kvs.at[:, span(i)], gc_r.at[i])
        store(kvs.at[:, span(i)], 1 - c, m, span(i))
    for i in late:
        columns = span(i)
        num_copies[i].wait_recv()
        result = val[c, :, columns].astype(F32) + (numer[i] + nrecv[:, columns]) * inverse
        out[:, columns] = jnp.where(live_mask, result / scale, 0.0)
    last = {}
    for i in late:
        place = kvx.at[:, span(i)]
        wait_for(place, gx_r.at[i])
        last[i] = send(place, kvxs.at[:, span(i)], gd_s, gd_r.at[i], {"parts": sibling})
        store(place, c, other, span(i))
    for i in late:
        last[i].wait_recv()
        store(kvxs.at[:, span(i)], 1 - c, other, span(i))

    wait_for(outgoing.at[pl.ds(0, n - 1)], halo_s)
    wait_for(outgoing, fwd_s)
    wait_for(stat.at[pl.ds(1, n - 1)], st_s)
    wait_for(ysend, y_s)
    wait_for(zrecv, z_s)
    wait_for(zrecv, g_s)
    wait_for(yrecv, gy_s)
    wait_for(kvx, gx_s)
    wait_for(kvs, gc_s)
    wait_for(kvx, gd_s)
    wait_for(nsend, num_s)
    for copy in (swap_feats, swap, *keys, values, *queries, den_swap):
        copy.wait_send()
    wait_for(kv_out, osem)


def fused(
    feats, adj_local, adj_halo, w_graph, w_query, w_key, w_value, send_rows, send_count, live
):
    n = lax.axis_size("parts")
    rows, cols = feats.shape
    slots = send_rows.shape[2]
    depth = w_graph.shape[0]
    half, piece = cols // 2, cols // 16
    quarter = half // 2
    chunks = ((0, 0, half), (0, half, half), (1, 0, half), (1, half, quarter), (1, half + quarter, quarter))
    count = len(chunks)
    vmem = pl.BlockSpec(memory_space=pltpu.VMEM)
    hbm = pl.BlockSpec(memory_space=pltpu.HBM)
    dma = pltpu.SemaphoreType.DMA
    place = functools.partial(pltpu.with_memory_space_constraint, memory_space=pltpu.HBM)
    out, kv = pl.pallas_call(
        functools.partial(kernel, n, chunks),
        out_shape=(
            jax.ShapeDtypeStruct((rows, cols), F32),
            jax.ShapeDtypeStruct((cols, depth), BF16),
        ),
        in_specs=[hbm] * 5 + [pl.BlockSpec(memory_space=pltpu.SMEM)] + [hbm] * 4,
        out_specs=(vmem, pl.BlockSpec(memory_space=pl.ANY)),
        scratch_shapes=[
            pltpu.VMEM((2, rows, cols), BF16),
            pltpu.VMEM(adj_local.shape, BF16),
            pltpu.VMEM(adj_halo.shape, BF16),
            pltpu.VMEM((slots, n), jnp.int32),
            pltpu.VMEM((1, n), jnp.int32),
            pltpu.VMEM((4, depth, cols), BF16),
            pltpu.VMEM((n, slots, cols), BF16),
            pltpu.VMEM((2, n, slots, cols), BF16),
            pltpu.VMEM((2, rows, cols), BF16),
            pltpu.VMEM((2, rows, cols), BF16),
            pltpu.VMEM((2, rows, cols), BF16),
            pltpu.VMEM((rows, cols), BF16),
            pltpu.VMEM((2, half, rows), BF16),
            pltpu.VMEM((2, 2, half, rows), BF16),
            pltpu.VMEM((2, rows, half), BF16),
            pltpu.VMEM((2, 2, rows, half), BF16),
            pltpu.VMEM((2, 2, 4 * piece, cols), F32),
            pltpu.VMEM((2, 4 * piece, cols), BF16),
            pltpu.VMEM((2, 4 * piece, cols), BF16),
            pltpu.VMEM((2, 4, piece, cols), F32),
            pltpu.VMEM((2, 4, piece, cols), BF16),
            pltpu.VMEM((2, 3, piece, cols), BF16),
            pltpu.VMEM((2, half, cols), BF16),
            pltpu.VMEM((half, cols), BF16),
            pltpu.VMEM((half, cols), BF16),
            pltpu.VMEM((half, cols), BF16),
            pltpu.VMEM((rows, cols), F32),
            pltpu.VMEM((rows, cols), F32),
            pltpu.VMEM((n, 1, cols + 128), F32),
            pltpu.VMEM((2, rows + 8, 128), F32),
            dma((5,)),
            dma((4,)),
            dma,
            dma((2,)),
            dma,
            dma((4,)),
            dma,
            dma,
            dma((2,)),
            dma((3,)),
            dma((3,)),
            dma((3,)),
            dma((3,)),
            dma((2,)),
            dma,
            dma((count,)),
            dma,
            dma((count,)),
            dma,
            dma((count,)),
            dma,
            dma((count, 3)),
            dma,
            dma((count,)),
            dma,
            dma((count,)),
            dma,
            dma((count,)),
            dma,
            dma((count,)),
            dma,
            dma,
            dma((2,)),
        ],
        compiler_params=pltpu.CompilerParams(
            collective_id=0, has_side_effects=True, vmem_limit_bytes=24 * 1024 * 1024
        ),
    )(
        *(place(a) for a in (feats, adj_local, adj_halo, send_rows[0].T, send_count)),
        live,
        *(place(w) for w in (w_graph, w_query, w_key, w_value)),
    )
    return out, kv.astype(F32) / math.sqrt(n * rows)


def local(*args):
    n = lax.axis_size("parts")
    rows, cols = args[0].shape
    slots = args[7].shape[2]
    fits = (
        lax.axis_size("mp") == 2
        and n == 16
        and cols % 512 == 0
        and rows % 128 == 0
        and (n * slots) % 16 == 0
        and slots % 8 == 0
    )
    return fused(*args) if fits else plain(*args)


def solution(mesh):
    return jax.shard_map(
        local,
        mesh=mesh,
        in_specs=(
            P("parts", "mp"),
            P("parts", None),
            P("parts", None),
            P(None, "mp"),
            P(None, "mp"),
            P(None, "mp"),
            P(None, "mp"),
            P("parts", None, None),
            P("parts", None),
            P("parts"),
        ),
        out_specs=(P("parts", "mp"), P("mp", None)),
        check_vma=False,
    )
```
